32 devices in a mesh: row: 4 (over y, core), col: 8 (over z, x).
Axes of the slice: x: 2, y: 2, z: 4, core: 2. Of those that a mesh axis runs over, the one named last changes fastest.
Arguments:
- current_left: bfloat16 [4, 128, 768, 128], P('row', 'col'), may hold values from -6 to 6
- current_right: bfloat16 [4, 128, 768, 128], P('row', 'col'), may hold values from -0.21875 to 0.21875
- current_rank: int32 [4, 128], P('row', 'col'), may hold values from 1 to 128
- target_rank: int32 [4, 128], P('row', 'col'), may hold values from 1 to 128
- update_left: bfloat16 [4, 64, 768, 128], P('row', 'col'), may hold values from -6 to 6
- update_right: bfloat16 [4, 64, 768, 128], P('row', 'col'), may hold values from -0.21875 to 0.21875
- update_rank: int32 [4, 64], P('row', 'col'), may hold values from 1 to 128
- owner_slot: int32 [4, 64], P('row', 'col'), may hold values from 0 to 127, as said below
Outputs:
- compressed_left: bfloat16 [4, 128, 768, 128], P('row', 'col')
- returned_right: bfloat16 [4, 64, 768, 128], P('row', 'col')
- row_scale: float32 [8, 768], P('row')
The draws below stay inside these ranges and needn't reach their ends.
Inputs may be any that keep to these rules, and one draw needn't show every extreme that they name: `owner_slot`: an entry is the tile's owning column index times 16 plus the tile's place on that owner. No tile is named by two contributions of its grid row. One device names either none or exactly 2 tiles of each owner. In every grid row some owner has all of its 16 tiles named.
All inputs are finite; a program needn't handle non-finite values.
Results may differ from the reference program's by a relative error of at most 0.0085.
Values may be sent and summed in bfloat16 or wider, within the bound.
A program may use at most 128 MiB of HBM per device.

```python
import math
import jax
import jax.numpy as jnp
from jax import lax

TILE = 768
HALF = 128
BR = 2
SWEEPS = 8
ROOTS = 3
SLOTS = 8
TILES_ROW = 128
CONTRIB_ROW = 64
N_ROW = 4
N_COL = 8


def owner_row(row_key):
    window_order = jax.random.permutation(jax.random.fold_in(row_key, 1), N_COL)
    swing_amount = jax.random.randint(jax.random.fold_in(row_key, 2), (N_COL // 2,), 0, SLOTS // 2 + 1)
    swing_amount = swing_amount.at[0].set(SLOTS // 2)
    pair_count = jnp.stack([SLOTS // 2 + swing_amount, SLOTS // 2 - swing_amount], axis=1).reshape(N_COL)
    window_start = jnp.cumsum(pair_count) - pair_count
    perm_keys = jax.random.split(jax.random.fold_in(row_key, 3), N_COL)
    tile_perms = jax.vmap(lambda one_key: jax.random.permutation(one_key, 2 * SLOTS))(perm_keys)
    tile_place = tile_perms.reshape(N_COL, SLOTS, 2)
    pair_index = jnp.arange(SLOTS)[None, :, None]
    is_valid = jnp.broadcast_to(pair_index < pair_count[:, None, None], (N_COL, SLOTS, 2))
    source = jnp.broadcast_to((window_start[:, None, None] + pair_index) % N_COL, (N_COL, SLOTS, 2))
    owner_col = jnp.broadcast_to(window_order[:, None, None], (N_COL, SLOTS, 2))
    slot_value = (owner_col * (2 * SLOTS) + tile_place).reshape(-1)
    entry_count = N_COL * SLOTS * 2
    flat_index = jnp.arange(entry_count)
    jitter = jax.random.randint(jax.random.fold_in(row_key, 4), (entry_count,), 0, 4096)
    score = jnp.where(is_valid.reshape(-1), source.reshape(-1) * (4096 * entry_count) + jitter * entry_count + flat_index, N_COL * 4096 * entry_count + flat_index)
    picked = jnp.argsort(score, stable=True)[:N_COL * SLOTS]
    return slot_value[picked].astype(jnp.int32)


def draw_owner_slot(key, part):
    row_keys = jax.random.split(jax.random.fold_in(key, 11), N_ROW)
    return jax.vmap(owner_row)(row_keys)


def set_ends(result, key, least, largest):
    spot = [jax.random.randint(jax.random.fold_in(key, axis), (), 0, length) for axis, length in enumerate(result.shape)]
    widest = result.shape.index(max(result.shape))
    neighbour = spot[:widest] + [(spot[widest] + 1) % result.shape[widest]] + spot[widest + 1:]
    return result.at[tuple(spot)].set(least).at[tuple(neighbour)].set(largest)


def shard_levels(own_key, dims, cuts, low, high):
    def one(axis_at, blocks):
        heights = jax.random.uniform(jax.random.fold_in(jax.random.fold_in(own_key, 6), axis_at), (blocks,), jnp.float32, low / len(cuts), high / len(cuts))
        return jnp.repeat(jnp.exp(heights), dims[axis_at] // blocks).reshape((-1,) + (1,) * (len(dims) - axis_at - 1))

    factor_of = one(*cuts[0])
    for cut in cuts[1:]:
        factor_of = factor_of * one(*cut)
    return factor_of


def normal_values(own_key, dims, spread, most, pieces=(), kind=jnp.bfloat16):
    values = jax.random.normal(own_key, dims, jnp.float32) * spread
    if len(pieces) > 0:
        values = shard_levels(own_key, dims, pieces, -0.22, 0.18) * values
    return jnp.clip(values, min=-most, max=most).astype(kind)


def setup_inputs(seed: int = 0) -> dict:
    streams_of = jax.random.split(jax.random.key(seed), 9)
    return {
        "current_left": normal_values(streams_of[0], (N_ROW, TILES_ROW, TILE, HALF), 1.0, 6.0, ((0, 4), (1, 8))),
        "current_right": normal_values(streams_of[1], (N_ROW, TILES_ROW, TILE, HALF), TILE ** -0.5, 0.21875, ((0, 4), (1, 8))),
        "current_rank": set_ends(jax.random.randint(streams_of[2], (N_ROW, TILES_ROW), 1, HALF + 1), jax.random.fold_in(streams_of[2], 1), 1, HALF).astype(jnp.int32),
        "target_rank": set_ends(jax.random.randint(streams_of[3], (N_ROW, TILES_ROW), 1, HALF + 1), jax.random.fold_in(streams_of[3], 1), 1, HALF).astype(jnp.int32),
        "update_left": normal_values(streams_of[4], (N_ROW, CONTRIB_ROW, TILE, HALF), 1.0, 6.0, ((0, 4), (1, 8))),
        "update_right": normal_values(streams_of[5], (N_ROW, CONTRIB_ROW, TILE, HALF), TILE ** -0.5, 0.21875, ((0, 4), (1, 8))),
        "update_rank": set_ends(jax.random.randint(streams_of[6], (N_ROW, CONTRIB_ROW), 1, HALF + 1), jax.random.fold_in(streams_of[6], 1), 1, HALF).astype(jnp.int32),
        "owner_slot": draw_owner_slot(jax.random.fold_in(streams_of[8], 71), 0),
    }


def high_dot(first, second):
    return jnp.dot(first, second, precision=lax.Precision.HIGHEST)

def square_roots(gram):
    order = gram.shape[0]
    identity = jnp.eye(order, dtype=jnp.float32)
    scale_value = jnp.sqrt(jnp.sum(gram * gram))
    root_now = gram / scale_value
    inverse_now = identity
    for repeat in range(ROOTS):
        middle = 1.5 * identity - 0.5 * high_dot(inverse_now, root_now)
        root_now = high_dot(root_now, middle)
        inverse_now = high_dot(middle, inverse_now)
    return (root_now * jnp.sqrt(scale_value), inverse_now / jnp.sqrt(scale_value))

def recompress(old_left, old_right, old_rank, add_left, add_right, add_rank, keep_rank):
    half_width = old_left.shape[1]
    column = jnp.arange(2 * half_width)
    live_mask = jnp.where(column < half_width, column < old_rank, column - half_width < add_rank).astype(jnp.float32)
    stack_left = jnp.concatenate([old_left, add_left], axis=1).astype(jnp.float32) * live_mask
    stack_right = jnp.concatenate([old_right, add_right], axis=1).astype(jnp.float32) * live_mask
    gram_left = high_dot(stack_left.T, stack_left)
    gram_right = high_dot(stack_right.T, stack_right) + jnp.diag(1.0 - live_mask)
    root_factor, inverse_factor = square_roots(gram_right)
    core_matrix = high_dot(high_dot(root_factor, gram_left), root_factor)
    subspace = core_matrix[:, :half_width] + core_matrix[:, half_width:]
    subspace = subspace / jnp.sqrt(jnp.sum(subspace * subspace) + 1e-06)
    for repeat in range(SWEEPS):
        inner = high_dot(subspace.T, subspace)
        subspace = 1.5 * subspace - 0.5 * high_dot(subspace, inner)
    subspace_kept = subspace * (jnp.arange(half_width) < keep_rank).astype(jnp.float32)
    new_left = high_dot(stack_left, high_dot(root_factor, subspace_kept))
    solved = high_dot(inverse_factor, subspace_kept)
    new_right = high_dot(stack_right, solved) * math.sqrt(stack_right.shape[0])
    return (new_left.astype(jnp.bfloat16), new_right.astype(jnp.bfloat16))

def reference(current_left, current_right, current_rank, target_rank, update_left, update_right, update_rank, owner_slot):
    row_count = current_rank.shape[0]
    tile_total = current_rank.shape[1]
    flat_tile = (owner_slot + jnp.arange(row_count, dtype=jnp.int32)[:, None] * tile_total).reshape(-1).astype(jnp.int32)
    tile_shape = current_left.shape[2:]
    flat_left = current_left.reshape((-1,) + tile_shape)
    flat_right = current_right.reshape((-1,) + tile_shape)
    items = (jnp.take(flat_left, flat_tile, axis=0), jnp.take(flat_right, flat_tile, axis=0), jnp.take(current_rank.reshape(-1), flat_tile), update_left.reshape((-1,) + tile_shape), update_right.reshape((-1,) + tile_shape), update_rank.reshape(-1), jnp.take(target_rank.reshape(-1), flat_tile))

    def single(entry):
        return recompress(*entry)
    new_left, new_right = lax.map(single, items)
    keep_cols = jnp.arange(HALF) < current_rank[:, :, None]
    masked = jnp.where(keep_cols[:, :, None, :], current_left, jnp.zeros((), current_left.dtype))
    compressed_left = masked.reshape((-1,) + tile_shape).at[flat_tile].set(new_left).reshape(current_left.shape)
    returned_right = new_right.reshape(update_left.shape)
    squares = lax.optimization_barrier(jnp.sum(jnp.square(compressed_left.astype(jnp.float32)), axis=3))
    row_sum = lax.optimization_barrier(jnp.sum(squares.reshape(row_count, tile_total // BR, BR, TILE), axis=1)).reshape(row_count * BR, TILE)
    mean_value = jnp.sum(row_sum) / (row_count * BR * TILE)
    row_scale = jnp.sqrt(row_sum / mean_value)
    return (compressed_left, returned_right, row_scale)
```

```python
import functools
import math

import jax
import jax.numpy as jnp
from jax import lax
from jax.experimental import pallas as pl
from jax.experimental.pallas import tpu as pltpu
from jax.sharding import PartitionSpec as P

CAP = 2
BR = 2
SWEEPS = 8
ROOTS = 3
F32 = jnp.float32
BF16 = jnp.bfloat16
HIGH = lax.Precision.HIGH


def bmm(a, b):
    return jnp.einsum("bij,bjk->bik", a, b, precision=HIGH, preferred_element_type=F32)


def contract_rows(a, b):
    return lax.dot_general(a, b, (((0,), (0,)), ((), ())), preferred_element_type=F32)


def gather_kernel(n, x_ref, o_ref, send_sem, recv_sem, own_sem):
    row, me = lax.axis_index("row"), lax.axis_index("col")
    barrier = pltpu.get_barrier_semaphore()
    for step in range(1, n):
        peer = lax.rem(me + step, n)
        pl.semaphore_signal(
            barrier, inc=1, device_id=(row, peer), device_id_type=pl.DeviceIdType.MESH
        )
    pl.semaphore_wait(barrier, n - 1)
    own = pltpu.make_async_copy(x_ref, o_ref.at[me], own_sem)
    own.start()
    copies = []
    for step in range(1, n):
        peer = lax.rem(me + step, n)
        copy = pltpu.make_async_remote_copy(
            src_ref=x_ref,
            dst_ref=o_ref.at[me],
            send_sem=send_sem.at[step],
            recv_sem=recv_sem.at[step],
            device_id=(row, peer),
            device_id_type=pl.DeviceIdType.MESH,
        )
        copy.start()
        copies.append(copy)
    own.wait()
    for copy in copies:
        copy.wait()


def gather_small(x, n):
    return pl.pallas_call(
        functools.partial(gather_kernel, n),
        out_shape=jax.ShapeDtypeStruct((n,) + x.shape, x.dtype),
        in_specs=[pl.BlockSpec(memory_space=pltpu.VMEM)],
        out_specs=pl.BlockSpec(memory_space=pltpu.VMEM),
        scratch_shapes=[
            pltpu.SemaphoreType.DMA((n,)),
            pltpu.SemaphoreType.DMA((n,)),
            pltpu.SemaphoreType.DMA,
        ],
        compiler_params=pltpu.CompilerParams(collective_id=0, has_side_effects=True),
        name="gather_small",
    )(x)


def scale_kernel(n, m, x_ref, o_ref, parts, mine, totals, sems, own_sem):
    send_a, recv_a, send_b, recv_b = (sems.at[i] for i in range(4))
    row, me = lax.axis_index("row"), lax.axis_index("col")
    barrier = pltpu.get_barrier_semaphore()
    for step in range(1, n):
        pl.semaphore_signal(
            barrier,
            inc=1,
            device_id=(row, lax.rem(me + step, n)),
            device_id_type=pl.DeviceIdType.MESH,
        )
    for step in range(1, m):
        pl.semaphore_signal(
            barrier,
            inc=1,
            device_id=(lax.rem(row + step, m), me),
            device_id_type=pl.DeviceIdType.MESH,
        )
    pl.semaphore_wait(barrier, n + m - 2)
    copies = []
    for step in range(1, n):
        copy = pltpu.make_async_remote_copy(
            src_ref=x_ref,
            dst_ref=parts.at[me],
            send_sem=send_a.at[step],
            recv_sem=recv_a.at[step],
            device_id=(row, lax.rem(me + step, n)),
            device_id_type=pl.DeviceIdType.MESH,
        )
        copy.start()
        copies.append(copy)
    own = pltpu.make_async_copy(x_ref, parts.at[me], own_sem.at[0])
    own.start()
    own.wait()
    for copy in copies:
        copy.wait()
    row_sum = jnp.sum(parts[...], axis=0)
    total = jnp.sum(jnp.sum(row_sum, axis=1, keepdims=True), axis=0, keepdims=True)
    mine[0] = jnp.broadcast_to(total, mine.shape[1:])
    fill = pltpu.make_async_copy(mine.at[0], mine.at[1], own_sem.at[1])
    fill.start()
    fill.wait()
    copies = []
    for step in range(1, m):
        copy = pltpu.make_async_remote_copy(
            src_ref=mine.at[1],
            dst_ref=totals.at[row],
            send_sem=send_b.at[step],
            recv_sem=recv_b.at[step],
            device_id=(lax.rem(row + step, m), me),
            device_id_type=pl.DeviceIdType.MESH,
        )
        copy.start()
        copies.append(copy)
    own = pltpu.make_async_copy(mine.at[1], totals.at[row], own_sem.at[0])
    own.start()
    own.wait()
    for copy in copies:
        copy.wait()
    everything = jnp.sum(totals[...], axis=0)[:1, :1]
    count = m * x_ref.shape[0] * x_ref.shape[1]
    o_ref[...] = jnp.sqrt(row_sum / (everything * (1.0 / count)))


def scale_rows(x, n, m):
    width = max(n, m)
    return pl.pallas_call(
        functools.partial(scale_kernel, n, m),
        out_shape=jax.ShapeDtypeStruct(x.shape, F32),
        in_specs=[pl.BlockSpec(memory_space=pltpu.VMEM)],
        out_specs=pl.BlockSpec(memory_space=pltpu.VMEM),
        scratch_shapes=[
            pltpu.VMEM((n,) + x.shape, F32),
            pltpu.VMEM((2, 8, 128), F32),
            pltpu.VMEM((m, 8, 128), F32),
            pltpu.SemaphoreType.DMA((4, width)),
            pltpu.SemaphoreType.DMA((2,)),
        ],
        compiler_params=pltpu.CompilerParams(collective_id=1, has_side_effects=True),
        name="scale_rows",
    )(x)


def owner_gram_kernel(tile_ref, cur_ref, upd_ref, o_ref):
    half = cur_ref.shape[1]
    o_ref[:, :half] = contract_rows(cur_ref[...], cur_ref[...]).astype(BF16)
    o_ref[:, half:] = contract_rows(cur_ref[...], upd_ref[...]).astype(BF16)


def owner_gram(asked, current, arrived):
    slots, order, half = arrived.shape
    return pl.pallas_call(
        owner_gram_kernel,
        grid_spec=pltpu.PrefetchScalarGridSpec(
            num_scalar_prefetch=1,
            grid=(slots,),
            in_specs=[
                pl.BlockSpec((None, order, half), lambda s, t: (t[s], 0, 0)),
                pl.BlockSpec((None, order, half), lambda s, t: (s, 0, 0)),
            ],
            out_specs=pl.BlockSpec((None, half, 2 * half), lambda s, t: (s, 0, 0)),
        ),
        out_shape=jax.ShapeDtypeStruct((slots, half, 2 * half), BF16),
        name="owner_gram",
    )(asked, current, arrived)


def owner_left_kernel(from_ref, hit_ref, rank_ref, cur_ref, upd_ref, mix_ref, o_ref, sum_ref):
    t = pl.program_id(0)
    half = cur_ref.shape[1]

    @pl.when(t == 0)
    def _():
        sum_ref[...] = jnp.zeros_like(sum_ref)

    @pl.when(hit_ref[t] > 0)
    def _():
        fresh = jnp.dot(cur_ref[...], mix_ref[:half], preferred_element_type=F32)
        fresh += jnp.dot(upd_ref[...], mix_ref[half:], preferred_element_type=F32)
        o_ref[...] = fresh.astype(BF16)

    @pl.when(hit_ref[t] == 0)
    def _():
        column = lax.broadcasted_iota(jnp.int32, cur_ref.shape, 1)
        o_ref[...] = jnp.where(
            column < rank_ref[t], cur_ref[...].astype(F32), 0.0
        ).astype(BF16)

    kept = o_ref[...].astype(F32)
    sums = lax.dot_general(
        jnp.ones((8, half), F32),
        kept * kept,
        (((1,), (1,)), ((), ())),
        precision=lax.Precision.HIGHEST,
        preferred_element_type=F32,
    )
    which = lax.broadcasted_iota(jnp.int32, sum_ref.shape, 0)
    sum_ref[...] += jnp.where(which == t % BR, sums[:BR], 0.0)


def owner_left(arrival, hit, rank, current, arrived, mix):
    tiles, order, half = current.shape
    return pl.pallas_call(
        owner_left_kernel,
        grid_spec=pltpu.PrefetchScalarGridSpec(
            num_scalar_prefetch=3,
            grid=(tiles,),
            in_specs=[
                pl.BlockSpec((None, order, half), lambda t, f, h, r: (t, 0, 0)),
                pl.BlockSpec((None, order, half), lambda t, f, h, r: (f[t], 0, 0)),
                pl.BlockSpec((None, 2 * half, half), lambda t, f, h, r: (f[t], 0, 0)),
            ],
            out_specs=[
                pl.BlockSpec((None, order, half), lambda t, f, h, r: (t, 0, 0)),
                pl.BlockSpec((BR, order), lambda t, f, h, r: (0, 0)),
            ],
        ),
        out_shape=[
            jax.ShapeDtypeStruct((tiles, order, half), BF16),
            jax.ShapeDtypeStruct((BR, order), F32),
        ],
        name="owner_left",
    )(arrival, hit, rank, current, arrived, mix)


def right_kernel(place_ref, cur_ref, upd_ref, mix_ref, o_ref):
    half = cur_ref.shape[1]
    fresh = jnp.dot(cur_ref[...], mix_ref[:half], preferred_element_type=F32)
    fresh += jnp.dot(upd_ref[...], mix_ref[half:], preferred_element_type=F32)
    o_ref[...] = fresh.astype(BF16)


def right_out(place, received, update, mix):
    slots, order, half = update.shape
    return pl.pallas_call(
        right_kernel,
        grid_spec=pltpu.PrefetchScalarGridSpec(
            num_scalar_prefetch=1,
            grid=(slots,),
            in_specs=[
                pl.BlockSpec((None, order, half), lambda j, p: (p[j], 0, 0)),
                pl.BlockSpec((None, order, half), lambda j, p: (j, 0, 0)),
                pl.BlockSpec((None, 2 * half, half), lambda j, p: (j, 0, 0)),
            ],
            out_specs=pl.BlockSpec((None, order, half), lambda j, p: (j, 0, 0)),
        ),
        out_shape=jax.ShapeDtypeStruct((slots, order, half), BF16),
        cost_estimate=pl.CostEstimate(
            flops=4 * slots * order * half * half,
            bytes_accessed=6 * slots * order * half,
            transcendentals=0,
        ),
        name="right_out",
    )(place, received, update, mix)


def right_gram_kernel(place_ref, cur_ref, upd_ref, o_ref):
    half = cur_ref.shape[1]
    cross = contract_rows(cur_ref[...], upd_ref[...])
    o_ref[:half, :half] = contract_rows(cur_ref[...], cur_ref[...])
    o_ref[:half, half:] = cross
    o_ref[half:, :half] = cross.T
    o_ref[half:, half:] = contract_rows(upd_ref[...], upd_ref[...])


def right_gram(place, received, update):
    slots, order, half = update.shape
    return pl.pallas_call(
        right_gram_kernel,
        grid_spec=pltpu.PrefetchScalarGridSpec(
            num_scalar_prefetch=1,
            grid=(slots,),
            in_specs=[
                pl.BlockSpec((None, order, half), lambda j, p: (p[j], 0, 0)),
                pl.BlockSpec((None, order, half), lambda j, p: (j, 0, 0)),
            ],
            out_specs=pl.BlockSpec((None, 2 * half, 2 * half), lambda j, p: (j, 0, 0)),
        ),
        out_shape=jax.ShapeDtypeStruct((slots, 2 * half, 2 * half), F32),
        name="right_gram",
    )(place, received, update)


def swap(values, n):
    shaped = values.reshape((n, CAP) + values.shape[1:])
    out = lax.all_to_all(shaped, "col", split_axis=0, concat_axis=0, tiled=True)
    return out.reshape(values.shape)


def take(values, index):
    return jnp.take(values, index, axis=0, mode="clip")


def local(
    current_left,
    current_right,
    current_rank,
    target_rank,
    update_left,
    update_right,
    update_rank,
    owner_slot,
):
    n = lax.axis_size("col")
    m = lax.axis_size("row")
    me = lax.axis_index("col")
    own_left, own_right = current_left[0], current_right[0]
    add_left, add_right = update_left[0], update_right[0]
    tiles, order, half = own_left.shape
    slots = owner_slot.shape[1]
    slot_index = jnp.arange(slots)

    mine = owner_slot[0]
    owner = mine // tiles
    earlier = (owner[:, None] == owner[None, :]) & (slot_index[None, :] < slot_index[:, None])
    place = owner * CAP + jnp.sum(earlier.astype(jnp.int32), axis=1)
    chosen = place[None, :] == jnp.arange(n * CAP)[:, None]
    source = jnp.sum(jnp.where(chosen, slot_index[None, :], 0), axis=1)
    arrived_left = swap(take(add_left, source), n)

    packed = jnp.concatenate([mine, current_rank[0], target_rank[0]])
    width = -(-packed.shape[0] // 128) * 128
    packed = jnp.pad(packed, (0, width - packed.shape[0])).reshape(1, width)
    table = gather_small(packed, n)[:, 0, :]
    named = table[:, :slots]
    ranks = table[:, slots : slots + tiles].reshape(-1)
    targets = table[:, slots + tiles : slots + 2 * tiles].reshape(-1)
    my_rank = jnp.sum(
        jnp.where(mine[:, None] == jnp.arange(n * tiles)[None, :], ranks[None, :], 0), axis=1
    )
    my_target = jnp.sum(
        jnp.where(mine[:, None] == jnp.arange(n * tiles)[None, :], targets[None, :], 0), axis=1
    )
    to_me = (named // tiles) == me
    count = jnp.sum(
        (to_me[:, None, :] & (slot_index[None, None, :] < slot_index[None, :, None])).astype(
            jnp.int32
        ),
        axis=2,
    )
    picked = to_me[:, None, :] & (count[:, None, :] == jnp.arange(CAP)[None, :, None])
    asked = jnp.sum(jnp.where(picked, (named % tiles)[:, None, :], 0), axis=2).reshape(-1)
    asked_used = jnp.any(picked, axis=2).reshape(-1)

    received_right = swap(take(own_right, asked), n)
    grams = swap(owner_gram(asked, own_left, arrived_left), n)

    column = jnp.arange(2 * half)[None, :]
    live = jnp.where(
        column < half, column < my_rank[:, None], column - half < update_rank[0][:, None]
    ).astype(F32)
    both = live[:, :, None] * live[:, None, :]
    identity = jnp.eye(2 * half, dtype=F32)
    gram_right = right_gram(place, received_right, add_right) * both
    gram_right = gram_right + identity * (1.0 - live)[:, :, None]
    c = jnp.sqrt(jnp.sum(gram_right * gram_right, axis=(1, 2), keepdims=True))
    root = gram_right / c
    inverse = 1.5 * identity - 0.5 * root
    root = bmm(root, inverse)
    for _ in range(ROOTS - 1):
        middle = 1.5 * identity - 0.5 * bmm(inverse, root)
        root = bmm(root, middle)
        inverse = bmm(middle, inverse)
    root = root * jnp.sqrt(c)
    inverse = inverse * lax.rsqrt(c)

    own_gram = jnp.einsum("bki,bkj->bij", add_left, add_left, preferred_element_type=F32)
    top = take(grams, place).astype(F32)
    low = jnp.concatenate([jnp.swapaxes(top[:, :, half:], 1, 2), own_gram], axis=2)
    gram_left = jnp.concatenate([top, low], axis=1) * both
    core = bmm(root, gram_left)
    core = bmm(core, root[:, :, :half] + root[:, :, half:])
    y = core * lax.rsqrt(jnp.sum(core * core, axis=(1, 2), keepdims=True) + 1e-06)
    for _ in range(SWEEPS):
        inner = jnp.einsum("bki,bkj->bij", y, y, precision=HIGH, preferred_element_type=F32)
        y = 1.5 * y - 0.5 * bmm(y, inner)
    y = y * (jnp.arange(half)[None, :] < my_target[:, None]).astype(F32)[:, None, :]
    mix_left = (bmm(root, y) * live[:, :, None]).astype(BF16)
    mix_right = (bmm(inverse, y) * (live[:, :, None] * math.sqrt(order))).astype(BF16)

    arrived_mix = swap(take(mix_left, source), n)
    returned_right = right_out(place, received_right, add_right, mix_right)

    matched = (asked[None, :] == jnp.arange(tiles)[:, None]) & asked_used[None, :]
    hit = jnp.any(matched, axis=1).astype(jnp.int32)
    arrival = jnp.sum(
        jnp.where(matched, jnp.arange(n * CAP)[None, :], 0), axis=1
    ).astype(jnp.int32)
    kept, partial = owner_left(
        arrival, hit, current_rank[0], own_left, arrived_left, arrived_mix
    )
    return (kept[None], returned_right[None], scale_rows(partial, n, m))


def solution(mesh):
    return jax.shard_map(
        local,
        mesh=mesh,
        in_specs=(
            P("row", "col", None, None),
            P("row", "col", None, None),
            P("row", "col"),
            P("row", "col"),
            P("row", "col", None, None),
            P("row", "col", None, None),
            P("row", "col"),
            P("row", "col"),
        ),
        out_specs=(P("row", "col", None, None), P("row", "col", None, None), P("row", None)),
        check_vma=False,
    )
```

```python
import functools
import math

import jax
import jax.numpy as jnp
from jax import lax
from jax.experimental import pallas as pl
from jax.experimental.pallas import tpu as pltpu
from jax.sharding import PartitionSpec as P

CAP = 2
BR = 2
SWEEPS = 8
ROOTS = 3
F32 = jnp.float32
BF16 = jnp.bfloat16


def contract_rows(a, b):
    return lax.dot_general(a, b, (((0,), (0,)), ((), ())), preferred_element_type=F32)


def gather_kernel(n, x_ref, o_ref, send_sem, recv_sem, own_sem):
    row, me = lax.axis_index("row"), lax.axis_index("col")
    barrier = pltpu.get_barrier_semaphore()
    for step in range(1, n):
        peer = lax.rem(me + step, n)
        pl.semaphore_signal(
            barrier, inc=1, device_id=(row, peer), device_id_type=pl.DeviceIdType.MESH
        )
    pl.semaphore_wait(barrier, n - 1)
    own = pltpu.make_async_copy(x_ref, o_ref.at[me], own_sem)
    own.start()
    copies = []
    for step in range(1, n):
        peer = lax.rem(me + step, n)
        copy = pltpu.make_async_remote_copy(
            src_ref=x_ref,
            dst_ref=o_ref.at[me],
            send_sem=send_sem.at[step],
            recv_sem=recv_sem.at[step],
            device_id=(row, peer),
            device_id_type=pl.DeviceIdType.MESH,
        )
        copy.start()
        copies.append(copy)
    own.wait()
    for copy in copies:
        copy.wait()


def gather_small(x, n):
    return pl.pallas_call(
        functools.partial(gather_kernel, n),
        out_shape=jax.ShapeDtypeStruct((n,) + x.shape, x.dtype),
        in_specs=[pl.BlockSpec(memory_space=pltpu.VMEM)],
        out_specs=pl.BlockSpec(memory_space=pltpu.VMEM),
        scratch_shapes=[
            pltpu.SemaphoreType.DMA((n,)),
            pltpu.SemaphoreType.DMA((n,)),
            pltpu.SemaphoreType.DMA,
        ],
        compiler_params=pltpu.CompilerParams(collective_id=0, has_side_effects=True),
        name="gather_small",
    )(x)


def scale_kernel(n, m, x_ref, o_ref, parts, mine, totals, sems, own_sem):
    send_a, recv_a, send_b, recv_b = (sems.at[i] for i in range(4))
    row, me = lax.axis_index("row"), lax.axis_index("col")
    barrier = pltpu.get_barrier_semaphore()
    for step in range(1, n):
        pl.semaphore_signal(
            barrier,
            inc=1,
            device_id=(row, lax.rem(me + step, n)),
            device_id_type=pl.DeviceIdType.MESH,
        )
    for step in range(1, m):
        pl.semaphore_signal(
            barrier,
            inc=1,
            device_id=(lax.rem(row + step, m), me),
            device_id_type=pl.DeviceIdType.MESH,
        )
    pl.semaphore_wait(barrier, n + m - 2)
    copies = []
    for step in range(1, n):
        copy = pltpu.make_async_remote_copy(
            src_ref=x_ref,
            dst_ref=parts.at[me],
            send_sem=send_a.at[step],
            recv_sem=recv_a.at[step],
            device_id=(row, lax.rem(me + step, n)),
            device_id_type=pl.DeviceIdType.MESH,
        )
        copy.start()
        copies.append(copy)
    own = pltpu.make_async_copy(x_ref, parts.at[me], own_sem.at[0])
    own.start()
    own.wait()
    for copy in copies:
        copy.wait()
    row_sum = jnp.sum(parts[...], axis=0)
    total = jnp.sum(jnp.sum(row_sum, axis=1, keepdims=True), axis=0, keepdims=True)
    mine[0] = jnp.broadcast_to(total, mine.shape[1:])
    fill = pltpu.make_async_copy(mine.at[0], mine.at[1], own_sem.at[1])
    fill.start()
    fill.wait()
    copies = []
    for step in range(1, m):
        copy = pltpu.make_async_remote_copy(
            src_ref=mine.at[1],
            dst_ref=totals.at[row],
            send_sem=send_b.at[step],
            recv_sem=recv_b.at[step],
            device_id=(lax.rem(row + step, m), me),
            device_id_type=pl.DeviceIdType.MESH,
        )
        copy.start()
        copies.append(copy)
    own = pltpu.make_async_copy(mine.at[1], totals.at[row], own_sem.at[0])
    own.start()
    own.wait()
    for copy in copies:
        copy.wait()
    everything = jnp.sum(totals[...], axis=0)[:1, :1]
    count = m * x_ref.shape[0] * x_ref.shape[1]
    o_ref[...] = jnp.sqrt(row_sum / (everything * (1.0 / count)))


def scale_rows(x, n, m):
    width = max(n, m)
    return pl.pallas_call(
        functools.partial(scale_kernel, n, m),
        out_shape=jax.ShapeDtypeStruct(x.shape, F32),
        in_specs=[pl.BlockSpec(memory_space=pltpu.VMEM)],
        out_specs=pl.BlockSpec(memory_space=pltpu.VMEM),
        scratch_shapes=[
            pltpu.VMEM((n,) + x.shape, F32),
            pltpu.VMEM((2, 8, 128), F32),
            pltpu.VMEM((m, 8, 128), F32),
            pltpu.SemaphoreType.DMA((4, width)),
            pltpu.SemaphoreType.DMA((2,)),
        ],
        compiler_params=pltpu.CompilerParams(collective_id=1, has_side_effects=True),
        name="scale_rows",
    )(x)


def split(a):
    upper = a.astype(BF16)
    return upper, (a - upper.astype(F32)).astype(BF16)


def product(a, b, dims=(((1,), (0,)), ((), ()))):
    dot = functools.partial(lax.dot_general, dimension_numbers=dims, preferred_element_type=F32)
    return dot(a[0], b[0]) + (dot(a[0], b[1]) + dot(a[1], b[0]))


def iota(shape, axis):
    return lax.broadcasted_iota(jnp.int32, shape, axis)


def total(a):
    return jnp.sum(jnp.sum(a, axis=1, keepdims=True), axis=0, keepdims=True)


def sweep_kernel(
    n,
    pairs,
    tab,
    send_left,
    send_right,
    own_left_hbm,
    add_left_hbm,
    add_right_hbm,
    got_left,
    got_mix,
    out_right,
    own_left,
    add_left,
    add_right,
    right_0,
    right_1,
    gram_send,
    gram_0,
    gram_1,
    roots,
    inverses,
    mixes,
    mix_send,
    sends,
    recvs,
    locals_,
):
    row, me = lax.axis_index("row"), lax.axis_index("col")
    order, half = got_left.shape[2:]
    wide = 2 * half
    slots = CAP * pairs
    at_tile, at_owner, at_index = 0, CAP * n, CAP * n + slots
    at_rank, at_add, at_keep = (CAP * n + i * slots for i in (2, 3, 4))
    at_pack = CAP * n + 5 * slots
    got_right = (right_0, right_1)
    got_gram = (gram_0, gram_1)

    loads = []
    for i, (src, dst) in enumerate(
        ((own_left_hbm, own_left), (add_left_hbm, add_left), (add_right_hbm, add_right))
    ):
        load = pltpu.make_async_copy(src, dst, locals_.at[8, i])
        load.start()
        loads.append(load)

    barrier = pltpu.get_barrier_semaphore()
    for step in range(1, n):
        pl.semaphore_signal(
            barrier,
            inc=1,
            device_id=(row, lax.rem(me + step, n)),
            device_id_type=pl.DeviceIdType.MESH,
        )
    pl.semaphore_wait(barrier, n - 1)

    def exchange(kind, src, dst):
        copies = []
        for step in [s for g in range(1, n // 2 + 1) for s in sorted({g, n - g})]:
            peer = lax.rem(me + step, n)
            copy = pltpu.make_async_remote_copy(
                src_ref=src(peer),
                dst_ref=dst(me),
                send_sem=sends.at[kind, step],
                recv_sem=recvs.at[kind, step],
                device_id=(row, peer),
                device_id_type=pl.DeviceIdType.MESH,
            )
            copy.start()
            copies.append(copy)
        own = pltpu.make_async_copy(src(me), dst(me), locals_.at[kind, 0])
        own.start()
        return own, copies

    def arrive(moved):
        moved[0].wait()
        for copy in moved[1]:
            copy.wait_recv()

    def sent(moved):
        for copy in moved[1]:
            copy.wait_send()

    def left_of(c):
        return exchange(c, lambda p: send_left.at[c, p], lambda p: got_left.at[c, p])

    def right_of(c):
        return exchange(2 + c, lambda p: send_right.at[c, p], lambda p: got_right[c].at[p])

    def gram_of(c):
        return exchange(4 + c, lambda p: gram_send.at[c, p], lambda p: got_gram[c].at[p])

    def mix_of(c):
        return exchange(6 + c, lambda p: mix_send.at[c, p], lambda p: got_mix.at[c, p])

    def masks(at):
        cur, add = tab[at_rank + at], tab[at_add + at]
        keeps = []
        for axis in (0, 1):
            i = iota((wide, wide), axis)
            keeps.append(((i < half) & (i < cur)) | ((i >= half) & (i - half < add)))
        return keeps[0] & keeps[1], keeps[0]

    def owner_grams(c):
        def one(d, _):
            cur = own_left[tab[at_tile + c * n + d]]
            both = jnp.concatenate([cur, got_left[c, d]], axis=1)
            gram_send[c, d] = contract_rows(cur, both).astype(BF16)
            return 0

        lax.fori_loop(0, n, one, 0)

    def right_stack(c, k):
        at = c * pairs + k
        return jnp.concatenate(
            [got_right[c][tab[at_owner + at]], add_right[tab[at_index + at]]], axis=1
        )

    def tile_roots(c, k):
        at = c * pairs + k
        stack = right_stack(c, k)
        keep, keep_row = masks(at)
        diagonal = iota((wide, wide), 0) == iota((wide, wide), 1)
        identity = jnp.where(diagonal, 1.0, 0.0).astype(F32)
        gram = jnp.where(keep, contract_rows(stack, stack), 0.0)
        gram = gram + jnp.where(diagonal & ~keep_row, 1.0, 0.0)
        scale = jnp.sqrt(total(gram * gram))
        root = gram * (1.0 / scale)
        inverse = 1.5 * identity - 0.5 * root
        root = product(split(root), split(inverse))
        for _ in range(ROOTS - 1):
            q, p = split(inverse), split(root)
            middle = split(1.5 * identity - 0.5 * product(q, p))
            root = product(p, middle)
            inverse = product(middle, q)
        roots[at] = root * jnp.sqrt(scale)
        inverses[at] = inverse * lax.rsqrt(scale)

    def tile_core(c, k):
        at = c * pairs + k
        top = got_gram[c][tab[at_owner + at]].astype(F32)
        add = add_left[tab[at_index + at]]
        low = jnp.concatenate([top[:, half:].T, contract_rows(add, add)], axis=1)
        gram = jnp.concatenate([top, low], axis=0)
        gram = jnp.where(masks(at)[0], gram, 0.0)
        root = roots[at]
        s = split(root)
        folded = root[:, :half] + root[:, half:]
        core = product(s, split(product(split(gram), split(folded))))
        y = core * lax.rsqrt(total(core * core) + 1e-06)
        for _ in range(SWEEPS):
            ys = split(y)
            inner = product(ys, ys, (((0,), (0,)), ((), ())))
            y = 1.5 * y - 0.5 * product(ys, split(inner))
        y = split(jnp.where(iota(y.shape, 1) < tab[at_keep + at], y, 0.0))
        mixes[at] = product(s, y).astype(BF16)
        mix = product(split(inverses[at]), y) * math.sqrt(order)
        return mix.astype(BF16)

    def each(c, work, many):
        def some(i, _):
            for j in range(many):
                work(c, i * many + j)
            return 0

        lax.fori_loop(0, pairs // many, some, 0)

    many = 2 if pairs % 2 == 0 else 1
    mixes_right = inverses

    def finish_core(c, k):
        mixes_right[c * pairs + k, :, :half] = tile_core(c, k).astype(F32)

    def right_out(c, k):
        at = c * pairs + k
        mix = mixes_right[at, :, :half].astype(BF16)
        out_right[at] = jnp.dot(
            right_stack(c, k), mix, preferred_element_type=F32
        ).astype(BF16)

    def pack(c):
        def one(o, _):
            mix_send[c, o] = mixes[tab[at_pack + c * n + o]]
            return 0

        lax.fori_loop(0, n, one, 0)

    left_a = left_of(0)
    right_a = right_of(0)
    left_b = left_of(1)
    for load in loads:
        load.wait()
    arrive(left_a)
    owner_grams(0)
    gram_a = gram_of(0)
    right_b = right_of(1)
    arrive(right_a)
    each(0, tile_roots, many)
    arrive(left_b)
    owner_grams(1)
    gram_b = gram_of(1)
    arrive(gram_a)
    each(0, finish_core, many)
    pack(0)
    mix_a = mix_of(0)
    each(0, right_out, many)
    arrive(right_b)
    each(1, tile_roots, many)
    arrive(gram_b)
    each(1, finish_core, many)
    pack(1)
    mix_b = mix_of(1)
    each(1, right_out, many)
    arrive(mix_a)
    arrive(mix_b)
    for moved in (left_a, right_a, left_b, gram_a, right_b, gram_b, mix_a, mix_b):
        sent(moved)


def sweep(tab, send_left, send_right, own_left, add_left, add_right, n):
    tiles, order, half = own_left.shape
    slots = add_left.shape[0]
    wide = 2 * half
    vmem = pl.BlockSpec(memory_space=pltpu.VMEM)
    hbm = pl.BlockSpec(memory_space=pl.ANY)
    return pl.pallas_call(
        functools.partial(sweep_kernel, n, slots // CAP),
        in_specs=[pl.BlockSpec(memory_space=pltpu.SMEM)] + [hbm] * 5,
        out_specs=[vmem] * 3,
        out_shape=[
            jax.ShapeDtypeStruct((CAP, n, order, half), BF16),
            jax.ShapeDtypeStruct((CAP, n, wide, half), BF16),
            jax.ShapeDtypeStruct((slots, order, half), BF16),
        ],
        scratch_shapes=[
            pltpu.VMEM((tiles, order, half), BF16),
            pltpu.VMEM((slots, order, half), BF16),
            pltpu.VMEM((slots, order, half), BF16),
            pltpu.VMEM((n, order, half), BF16),
            pltpu.VMEM((n, order, half), BF16),
            pltpu.VMEM((CAP, n, half, wide), BF16),
            pltpu.VMEM((n, half, wide), BF16),
            pltpu.VMEM((n, half, wide), BF16),
            pltpu.VMEM((slots, wide, wide), F32),
            pltpu.VMEM((slots, wide, wide), F32),
            pltpu.VMEM((slots, wide, half), BF16),
            pltpu.VMEM((CAP, n, wide, half), BF16),
            pltpu.SemaphoreType.DMA((8, n)),
            pltpu.SemaphoreType.DMA((8, n)),
            pltpu.SemaphoreType.DMA((9, 3)),
        ],
        compiler_params=pltpu.CompilerParams(
            collective_id=2, has_side_effects=True, vmem_limit_bytes=60 * 1024 * 1024
        ),
        name="sweep",
    )(tab, send_left, send_right, own_left, add_left, add_right)


def owner_left_kernel(from_ref, hit_ref, rank_ref, cur_ref, upd_ref, mix_ref, o_ref, sum_ref):
    t = pl.program_id(0)
    half = cur_ref.shape[1]

    @pl.when(t == 0)
    def _():
        sum_ref[...] = jnp.zeros_like(sum_ref)

    @pl.when(hit_ref[t] > 0)
    def _():
        fresh = jnp.dot(cur_ref[...], mix_ref[:half], preferred_element_type=F32)
        fresh += jnp.dot(upd_ref[...], mix_ref[half:], preferred_element_type=F32)
        o_ref[...] = fresh.astype(BF16)

    @pl.when(hit_ref[t] == 0)
    def _():
        column = lax.broadcasted_iota(jnp.int32, cur_ref.shape, 1)
        o_ref[...] = jnp.where(
            column < rank_ref[t], cur_ref[...].astype(F32), 0.0
        ).astype(BF16)

    kept = o_ref[...].astype(F32)
    sums = lax.dot_general(
        jnp.ones((8, half), F32),
        kept * kept,
        (((1,), (1,)), ((), ())),
        precision=lax.Precision.HIGHEST,
        preferred_element_type=F32,
    )
    which = lax.broadcasted_iota(jnp.int32, sum_ref.shape, 0)
    sum_ref[...] += jnp.where(which == t % BR, sums[:BR], 0.0)


def owner_left(arrival, hit, rank, current, arrived, mix):
    tiles, order, half = current.shape
    return pl.pallas_call(
        owner_left_kernel,
        grid_spec=pltpu.PrefetchScalarGridSpec(
            num_scalar_prefetch=3,
            grid=(tiles,),
            in_specs=[
                pl.BlockSpec((None, order, half), lambda t, f, h, r: (t, 0, 0)),
                pl.BlockSpec((None, order, half), lambda t, f, h, r: (f[t], 0, 0)),
                pl.BlockSpec((None, 2 * half, half), lambda t, f, h, r: (f[t], 0, 0)),
            ],
            out_specs=[
                pl.BlockSpec((None, order, half), lambda t, f, h, r: (t, 0, 0)),
                pl.BlockSpec((BR, order), lambda t, f, h, r: (0, 0)),
            ],
        ),
        out_shape=[
            jax.ShapeDtypeStruct((tiles, order, half), BF16),
            jax.ShapeDtypeStruct((BR, order), F32),
        ],
        name="owner_left",
    )(arrival, hit, rank, current, arrived, mix)


def take(values, index):
    return jnp.take(values, index, axis=0, mode="clip")


def pick(mask, values):
    return jnp.sum(jnp.where(mask, values, 0), axis=-1).astype(jnp.int32)


def local(
    current_left,
    current_right,
    current_rank,
    target_rank,
    update_left,
    update_right,
    update_rank,
    owner_slot,
):
    n = lax.axis_size("col")
    m = lax.axis_size("row")
    me = lax.axis_index("col")
    own_left, own_right = current_left[0], current_right[0]
    add_left, add_right = update_left[0], update_right[0]
    tiles, order, half = own_left.shape
    slots = owner_slot.shape[1]
    pairs = slots // CAP
    slot_index = jnp.arange(slots)

    mine = owner_slot[0]
    owner = mine // tiles
    which = pick(
        (owner[:, None] == owner[None, :]) & (slot_index[None, :] < slot_index[:, None]), 1
    )
    place = which * n + owner
    chosen = place[None, :] == jnp.arange(CAP * n)[:, None]
    source = pick(chosen, slot_index[None, :])
    send_left = take(add_left, source).reshape((CAP, n, order, half))
    rank_in = pick(place[None, :] < place[:, None], 1)
    to_slot = pick(rank_in[None, :] == slot_index[:, None], slot_index[None, :])
    pack = pick(chosen, rank_in[None, :])

    packed = jnp.concatenate([mine, current_rank[0], target_rank[0]])
    width = -(-packed.shape[0] // 128) * 128
    packed = jnp.pad(packed, (0, width - packed.shape[0])).reshape(1, width)
    table = gather_small(packed, n)[:, 0, :]
    named = table[:, :slots]
    ranks = table[:, slots : slots + tiles].reshape(-1)
    targets = table[:, slots + tiles : slots + 2 * tiles].reshape(-1)
    of_mine = mine[:, None] == jnp.arange(n * tiles)[None, :]
    per_slot = jnp.stack(
        [
            owner,
            slot_index,
            pick(of_mine, ranks[None, :]),
            update_rank[0],
            pick(of_mine, targets[None, :]),
        ]
    )
    in_order = pick((to_slot[:, None] == slot_index[None, :])[None], per_slot[:, None, :])
    to_me = (named // tiles) == me
    count = pick(
        to_me[:, None, :] & (slot_index[None, None, :] < slot_index[None, :, None]), 1
    )
    picked = to_me[None] & (count[None] == jnp.arange(CAP)[:, None, None])
    asked = pick(picked, (named % tiles)[None]).reshape(-1)
    asked_used = jnp.any(picked, axis=2).reshape(-1)
    send_right = take(own_right, asked).reshape((CAP, n, order, half))

    tab = jnp.concatenate([asked, in_order.reshape(-1), pack])
    arrived_left, arrived_mix, right = sweep(
        tab, send_left, send_right, own_left, add_left, add_right, n
    )
    returned_right = take(right, rank_in)

    matched = (asked[None, :] == jnp.arange(tiles)[:, None]) & asked_used[None, :]
    hit = jnp.any(matched, axis=1).astype(jnp.int32)
    arrival = pick(matched, jnp.arange(n * CAP)[None, :])
    kept, partial = owner_left(
        arrival,
        hit,
        current_rank[0],
        own_left,
        arrived_left.reshape((CAP * n, order, half)),
        arrived_mix.reshape((CAP * n, 2 * half, half)),
    )
    return (kept[None], returned_right[None], scale_rows(partial, n, m))


def solution(mesh):
    return jax.shard_map(
        local,
        mesh=mesh,
        in_specs=(
            P("row", "col", None, None),
            P("row", "col", None, None),
            P("row", "col"),
            P("row", "col"),
            P("row", "col", None, None),
            P("row", "col", None, None),
            P("row", "col"),
            P("row", "col"),
        ),
        out_specs=(P("row", "col", None, None), P("row", "col", None, None), P("row", None)),
        check_vma=False,
    )
```

```python
import functools
import math

import jax
import jax.numpy as jnp
from jax import lax
from jax.experimental import pallas as pl
from jax.experimental.pallas import tpu as pltpu
from jax.sharding import PartitionSpec as P

CAP = 2
BR = 2
SWEEPS = 8
ROOTS = 3
F32 = jnp.float32
BF16 = jnp.bfloat16


def contract_rows(a, b):
    return lax.dot_general(a, b, (((0,), (0,)), ((), ())), preferred_element_type=F32)


def split(a):
    upper = a.astype(BF16)
    return upper, (a - upper.astype(F32)).astype(BF16)


def product(a, b, dims=(((1,), (0,)), ((), ()))):
    dot = functools.partial(lax.dot_general, dimension_numbers=dims, preferred_element_type=F32)
    return dot(a[0], b[0]) + (dot(a[0], b[1]) + dot(a[1], b[0]))


def iota(shape, axis):
    return lax.broadcasted_iota(jnp.int32, shape, axis)


def total(a):
    return jnp.sum(jnp.sum(a, axis=1, keepdims=True), axis=0, keepdims=True)


def sweep_kernel(
    n,
    m,
    mine,
    packed,
    own_left_hbm,
    own_right_hbm,
    add_left_hbm,
    add_right_hbm,
    kept_left,
    out_right,
    out_scale,
    own_left,
    own_right,
    add_left,
    add_right,
    send_left,
    send_right,
    got_left,
    right_0,
    right_1,
    gram_send,
    gram_0,
    gram_1,
    roots,
    inverses,
    mixes,
    mix_send,
    got_mix,
    made_right,
    squares,
    rows,
    parts,
    mine_total,
    totals,
    table_vmem,
    table,
    tab,
    sends,
    recvs,
    row_sems,
    locals_,
):
    row, me = lax.axis_index("row"), lax.axis_index("col")
    order, half = got_left.shape[2:]
    wide = 2 * half
    tiles, slots = own_left.shape[0], add_left.shape[0]
    pairs = slots // CAP
    at_tile, at_source, at_used, at_seq, at_has = 0, CAP * n, 2 * CAP * n, 3 * CAP * n, 4 * CAP * n
    at_owner, at_index, at_rank, at_add, at_keep = (5 * CAP * n + i * slots for i in range(5))
    at_arrival = 5 * CAP * n + 5 * slots
    at_hit = at_arrival + tiles
    got_right = (right_0, right_1)
    got_gram = (gram_0, gram_1)

    loads = []
    for i, (src, dst) in enumerate(
        (
            (add_left_hbm, add_left),
            (own_right_hbm, own_right),
            (own_left_hbm, own_left),
            (add_right_hbm, add_right),
        )
    ):
        load = pltpu.make_async_copy(src, dst, locals_.at[9, i])
        load.start()
        loads.append(load)

    barrier = pltpu.get_barrier_semaphore()
    for step in range(1, n):
        pl.semaphore_signal(
            barrier,
            inc=1,
            device_id=(row, lax.rem(me + step, n)),
            device_id_type=pl.DeviceIdType.MESH,
        )
    for step in range(1, m):
        pl.semaphore_signal(
            barrier,
            inc=1,
            device_id=(lax.rem(row + step, m), me),
            device_id_type=pl.DeviceIdType.MESH,
        )

    def slots_of(owner, held):
        count, found = jnp.int32(0), [jnp.int32(0)] * CAP
        for j in range(slots):
            hit = lax.div(held(j), tiles) == owner
            for c in range(CAP):
                found[c] = jnp.where(hit & (count == c), j, found[c])
            count = count + jnp.where(hit, 1, 0)
        return jnp.where(count > 0, 1, 0), found

    def my_owner(o, before):
        has, found = slots_of(o, lambda j: mine[0, j])
        for c in range(CAP):
            tab[at_source + c * n + o] = found[c]
        tab[at_seq + o] = jnp.minimum(before, pairs - 1)
        tab[at_has + o] = has
        return before + has

    lax.fori_loop(0, n, my_owner, jnp.int32(0))

    def pack_left(c):
        def one(o, _):
            send_left[c, o] = add_left[tab[at_source + c * n + o]]
            return 0

        lax.fori_loop(0, n, one, 0)

    loads[0].wait()
    pack_left(0)
    pack_left(1)
    pl.semaphore_wait(barrier, n + m - 2)

    def exchange(kind, src, dst):
        copies = []
        for step in [s for g in range(1, n // 2 + 1) for s in sorted({g, n - g})]:
            peer = lax.rem(me + step, n)
            copy = pltpu.make_async_remote_copy(
                src_ref=src(peer),
                dst_ref=dst(me),
                send_sem=sends.at[kind, step],
                recv_sem=recvs.at[kind, step],
                device_id=(row, peer),
                device_id_type=pl.DeviceIdType.MESH,
            )
            copy.start()
            copies.append(copy)
        own = pltpu.make_async_copy(src(me), dst(me), locals_.at[kind, 0])
        own.start()
        return own, copies

    def arrive(moved):
        moved[0].wait()
        for copy in moved[1]:
            copy.wait_recv()

    def sent(moved):
        for copy in moved[1]:
            copy.wait_send()

    def row_of(p):
        return table_vmem.at[p]

    def left_of(c):
        return exchange(c, lambda p: send_left.at[c, p], lambda p: got_left.at[c, p])

    def right_of(c):
        return exchange(2 + c, lambda p: send_right.at[c, p], lambda p: got_right[c].at[p])

    def gram_of(c):
        return exchange(4 + c, lambda p: gram_send.at[c, p], lambda p: got_gram[c].at[p])

    def mix_of(c):
        return exchange(6 + c, lambda p: mix_send.at[c, p], lambda p: got_mix.at[c, p])

    def masks(at):
        cur, add = tab[at_rank + at], tab[at_add + at]
        keeps = []
        for axis in (0, 1):
            i = iota((wide, wide), axis)
            keeps.append(((i < half) & (i < cur)) | ((i >= half) & (i - half < add)))
        return keeps[0] & keeps[1], keeps[0]

    def owner_grams(c):
        def one(d, _):
            cur = own_left[tab[at_tile + c * n + d]]
            both = jnp.concatenate([cur, got_left[c, d]], axis=1)
            gram_send[c, d] = contract_rows(cur, both).astype(BF16)
            return 0

        lax.fori_loop(0, n, one, 0)

    def right_stack(c, k):
        at = c * pairs + k
        return jnp.concatenate(
            [got_right[c][tab[at_owner + at]], add_right[tab[at_index + at]]], axis=1
        )

    def tile_roots(c, k):
        at = c * pairs + k
        stack = right_stack(c, k)
        keep, keep_row = masks(at)
        diagonal = iota((wide, wide), 0) == iota((wide, wide), 1)
        identity = jnp.where(diagonal, 1.0, 0.0).astype(F32)
        gram = jnp.where(keep, contract_rows(stack, stack), 0.0)
        gram = gram + jnp.where(diagonal & ~keep_row, 1.0, 0.0)
        scale = jnp.sqrt(total(gram * gram))
        root = gram * (1.0 / scale)
        inverse = 1.5 * identity - 0.5 * root
        root = product(split(root), split(inverse))
        for _ in range(ROOTS - 1):
            q, p = split(inverse), split(root)
            middle = split(1.5 * identity - 0.5 * product(q, p))
            root = product(p, middle)
            inverse = product(middle, q)
        roots[at] = root * jnp.sqrt(scale)
        inverses[at] = inverse * lax.rsqrt(scale)

    def tile_core(c, k):
        at = c * pairs + k
        top = got_gram[c][tab[at_owner + at]].astype(F32)
        add = add_left[tab[at_index + at]]
        low = jnp.concatenate([top[:, half:].T, contract_rows(add, add)], axis=1)
        gram = jnp.concatenate([top, low], axis=0)
        gram = jnp.where(masks(at)[0], gram, 0.0)
        root = roots[at]
        s = split(root)
        folded = root[:, :half] + root[:, half:]
        core = product(s, split(product(split(gram), split(folded))))
        y = core * lax.rsqrt(total(core * core) + 1e-06)
        for _ in range(SWEEPS):
            ys = split(y)
            inner = product(ys, ys, (((0,), (0,)), ((), ())))
            y = 1.5 * y - 0.5 * product(ys, split(inner))
        y = split(jnp.where(iota(y.shape, 1) < tab[at_keep + at], y, 0.0))
        mixes[at] = product(s, y).astype(BF16)
        mix = product(split(inverses[at]), y) * math.sqrt(order)
        return mix.astype(BF16)

    def each(c, work, many):
        def some(i, _):
            for j in range(many):
                work(c, i * many + j)
            return 0

        lax.fori_loop(0, pairs // many, some, 0)

    many = 2 if pairs % 2 == 0 else 1
    mixes_right = inverses

    def finish_core(c, k):
        mixes_right[c * pairs + k, :, :half] = tile_core(c, k).astype(F32)

    def right_out(c, k):
        at = c * pairs + k
        mix = mixes_right[at, :, :half].astype(BF16)
        made_right[at] = jnp.dot(
            right_stack(c, k), mix, preferred_element_type=F32
        ).astype(BF16)

    def pack(c):
        def one(o, _):
            mix_send[c, o] = mixes[c * pairs + tab[at_seq + o]]
            return 0

        lax.fori_loop(0, n, one, 0)

    def index_tables():
        for k in range(pairs):

            def one(o, found):
                chosen = (tab[at_has + o] > 0) & (tab[at_seq + o] == k)
                new = [o] + [tab[at_source + c * n + o] for c in range(CAP)]
                return tuple(jnp.where(chosen, a, b) for a, b in zip(new, found))

            found = lax.fori_loop(0, n, one, (jnp.int32(0),) * (CAP + 1))
            for c in range(CAP):
                at, j = c * pairs + k, found[1 + c]
                tile = lax.rem(mine[0, j], tiles)
                tab[at_owner + at] = found[0]
                tab[at_index + at] = j
                tab[at_rank + at] = table[found[0], 0, slots + tile]
                tab[at_keep + at] = table[found[0], 0, slots + tiles + tile]
                tab[at_add + at] = mine[0, slots + 2 * tiles + j]

    def asked_tables():
        def one(d, _):
            has, found = slots_of(me, lambda j: table[d, 0, j])
            for c in range(CAP):
                tab[at_tile + c * n + d] = lax.rem(table[d, 0, found[c]], tiles)
                tab[at_used + c * n + d] = has
            return 0

        lax.fori_loop(0, n, one, 0)

    def arrival_tables():
        def tile(t, _):
            def one(s, found):
                hit = (tab[at_tile + s] == t) & (tab[at_used + s] > 0)
                return jnp.where(hit, s, found[0]), jnp.where(hit, 1, found[1])

            found = lax.fori_loop(0, CAP * n, one, (jnp.int32(0), jnp.int32(0)))
            tab[at_arrival + t] = found[0]
            tab[at_hit + t] = found[1]
            return 0

        lax.fori_loop(0, tiles, tile, 0)

    def pack_right():
        def one(d, _):
            for c in range(CAP):
                send_right[c, d] = own_right[tab[at_tile + c * n + d]]
            return 0

        lax.fori_loop(0, n, one, 0)

    fresh = send_right

    def new_left(c):
        def one(d, _):
            both = jnp.concatenate([own_left[tab[at_tile + c * n + d]], got_left[c, d]], axis=1)
            made = jnp.dot(both, got_mix[c, d], preferred_element_type=F32)
            fresh[c, d] = made.astype(BF16)
            return 0

        lax.fori_loop(0, n, one, 0)

    def keep_tiles():
        squares[...] = jnp.zeros_like(squares)

        def one(i, _):
            for b in range(BR):
                t = i * BR + b
                s = tab[at_arrival + t]
                hit = tab[at_hit + t] > 0
                limit = jnp.where(hit, 0, mine[0, slots + t])
                column = iota((order, half), 1)
                old = jnp.where(column < limit, own_left[t].astype(F32), 0.0)
                new = fresh[lax.div(s, n), lax.rem(s, n)].astype(F32)
                kept = jnp.where(hit, new, old)
                kept_left[t] = kept.astype(BF16)
                squares[b] += kept * kept
            return 0

        lax.fori_loop(0, tiles // BR, one, 0)
        for b in range(BR):
            sums = lax.dot_general(
                jnp.ones((8, half), F32),
                squares[b],
                (((1,), (1,)), ((), ())),
                precision=lax.Precision.HIGHEST,
                preferred_element_type=F32,
            )
            rows[0, b : b + 1] = sums[:1]

    def local_copy(src, dst, i):
        copy = pltpu.make_async_copy(src, dst, locals_.at[10, i])
        copy.start()
        copy.wait()

    def scale_rows():
        local_copy(rows.at[0], rows.at[1], 0)
        moved = exchange(9, lambda p: rows.at[1], lambda p: parts.at[p])
        arrive(moved)
        row_sum = jnp.sum(parts[...], axis=0)
        mine_total[0] = jnp.broadcast_to(total(row_sum), mine_total.shape[1:])
        local_copy(mine_total.at[0], mine_total.at[1], 1)
        copies = []
        for step in range(1, m):
            copy = pltpu.make_async_remote_copy(
                src_ref=mine_total.at[1],
                dst_ref=totals.at[row],
                send_sem=row_sems.at[0, step],
                recv_sem=row_sems.at[1, step],
                device_id=(lax.rem(row + step, m), me),
                device_id_type=pl.DeviceIdType.MESH,
            )
            copy.start()
            copies.append(copy)
        local_copy(mine_total.at[1], totals.at[row], 2)
        for copy in copies:
            copy.wait()
        everything = jnp.sum(totals[...], axis=0)[:1, :1]
        out_scale[...] = jnp.sqrt(row_sum / (everything * (1.0 / (m * BR * order))))
        sent(moved)

    routes = exchange(8, lambda p: packed, row_of)
    left_a = left_of(0)
    arrive(routes)
    local_copy(table_vmem, table, 3)
    asked_tables()
    loads[1].wait()
    pack_right()
    right_a = right_of(0)
    left_b = left_of(1)
    index_tables()
    arrival_tables()
    loads[2].wait()
    loads[3].wait()
    arrive(left_a)
    owner_grams(0)
    gram_a = gram_of(0)
    right_b = right_of(1)
    arrive(right_a)
    each(0, tile_roots, many)
    arrive(left_b)
    owner_grams(1)
    gram_b = gram_of(1)
    arrive(gram_a)
    each(0, finish_core, many)
    pack(0)
    mix_a = mix_of(0)
    each(0, right_out, many)
    arrive(right_b)
    each(1, tile_roots, many)
    arrive(gram_b)
    each(1, finish_core, many)
    pack(1)
    mix_b = mix_of(1)
    each(1, right_out, many)
    for j in range(slots):
        o = lax.div(mine[0, j], tiles)
        first = tab[at_source + o] == j
        out_right[j] = made_right[tab[at_seq + o] + jnp.where(first, 0, pairs)]
    sent(right_a)
    sent(right_b)
    arrive(mix_a)
    new_left(0)
    arrive(mix_b)
    new_left(1)
    keep_tiles()
    scale_rows()
    for moved in (routes, left_a, left_b, gram_a, gram_b, mix_a, mix_b):
        sent(moved)


def sweep(packed, own_left, own_right, add_left, add_right, n, m):
    tiles, order, half = own_left.shape
    slots = add_left.shape[0]
    wide = 2 * half
    vmem = pl.BlockSpec(memory_space=pltpu.VMEM)
    hbm = pl.BlockSpec(memory_space=pl.ANY)
    entries = 5 * CAP * n + 5 * slots + 2 * tiles
    return pl.pallas_call(
        functools.partial(sweep_kernel, n, m),
        in_specs=[pl.BlockSpec(memory_space=pltpu.SMEM), vmem] + [hbm] * 4,
        out_specs=[vmem] * 3,
        out_shape=[
            jax.ShapeDtypeStruct((tiles, order, half), BF16),
            jax.ShapeDtypeStruct((slots, order, half), BF16),
            jax.ShapeDtypeStruct((BR, order), F32),
        ],
        scratch_shapes=[
            pltpu.VMEM((tiles, order, half), BF16),
            pltpu.VMEM((tiles, order, half), BF16),
            pltpu.VMEM((slots, order, half), BF16),
            pltpu.VMEM((slots, order, half), BF16),
            pltpu.VMEM((CAP, n, order, half), BF16),
            pltpu.VMEM((CAP, n, order, half), BF16),
            pltpu.VMEM((CAP, n, order, half), BF16),
            pltpu.VMEM((n, order, half), BF16),
            pltpu.VMEM((n, order, half), BF16),
            pltpu.VMEM((CAP, n, half, wide), BF16),
            pltpu.VMEM((n, half, wide), BF16),
            pltpu.VMEM((n, half, wide), BF16),
            pltpu.VMEM((slots, wide, wide), F32),
            pltpu.VMEM((slots, wide, wide), F32),
            pltpu.VMEM((slots, wide, half), BF16),
            pltpu.VMEM((CAP, n, wide, half), BF16),
            pltpu.VMEM((CAP, n, wide, half), BF16),
            pltpu.VMEM((slots, order, half), BF16),
            pltpu.VMEM((BR, order, half), F32),
            pltpu.VMEM((2, BR, order), F32),
            pltpu.VMEM((n, BR, order), F32),
            pltpu.VMEM((2, 8, 128), F32),
            pltpu.VMEM((m, 8, 128), F32),
            pltpu.VMEM((n,) + packed.shape, jnp.int32),
            pltpu.SMEM((n,) + packed.shape, jnp.int32),
            pltpu.SMEM((entries,), jnp.int32),
            pltpu.SemaphoreType.DMA((10, n)),
            pltpu.SemaphoreType.DMA((10, n)),
            pltpu.SemaphoreType.DMA((2, m)),
            pltpu.SemaphoreType.DMA((11, 4)),
        ],
        compiler_params=pltpu.CompilerParams(
            collective_id=0, has_side_effects=True, vmem_limit_bytes=62 * 1024 * 1024
        ),
        name="sweep",
    )(packed, packed, own_left, own_right, add_left, add_right)


def local(
    current_left,
    current_right,
    current_rank,
    target_rank,
    update_left,
    update_right,
    update_rank,
    owner_slot,
):
    packed = jnp.concatenate([owner_slot, current_rank, target_rank, update_rank], axis=1)
    width = -(-packed.shape[1] // 128) * 128
    packed = jnp.pad(packed, ((0, 0), (0, width - packed.shape[1])))
    kept, right, scale = sweep(
        packed,
        current_left[0],
        current_right[0],
        update_left[0],
        update_right[0],
        lax.axis_size("col"),
        lax.axis_size("row"),
    )
    return (kept[None], right[None], scale)


def solution(mesh):
    return jax.shard_map(
        local,
        mesh=mesh,
        in_specs=(
            P("row", "col", None, None),
            P("row", "col", None, None),
            P("row", "col"),
            P("row", "col"),
            P("row", "col", None, None),
            P("row", "col", None, None),
            P("row", "col"),
            P("row", "col"),
        ),
        out_specs=(P("row", "col", None, None), P("row", "col", None, None), P("row", None)),
        check_vma=False,
    )
```

```python
import functools
import math

import jax
import jax.numpy as jnp
from jax import lax
from jax.experimental import pallas as pl
from jax.experimental.pallas import tpu as pltpu
from jax.sharding import PartitionSpec as P

CAP = 2
BR = 2
SWEEPS = 8
FINE = 2
ROOTS = 3
F32 = jnp.float32
BF16 = jnp.bfloat16


def contract_rows(a, b):
    return lax.dot_general(a, b, (((0,), (0,)), ((), ())), preferred_element_type=F32)


def split(a):
    upper = a.astype(BF16)
    return upper, (a - upper.astype(F32)).astype(BF16)


def product(a, b, dims=(((1,), (0,)), ((), ()))):
    dot = functools.partial(lax.dot_general, dimension_numbers=dims, preferred_element_type=F32)
    return dot(a[0], b[0]) + (dot(a[0], b[1]) + dot(a[1], b[0]))


def iota(shape, axis):
    return lax.broadcasted_iota(jnp.int32, shape, axis)


def total(a):
    return jnp.sum(jnp.sum(a, axis=1, keepdims=True), axis=0, keepdims=True)


def sweep_kernel(
    n,
    m,
    mine,
    packed,
    own_left_hbm,
    own_right_hbm,
    add_left_hbm,
    add_right_hbm,
    kept_left,
    out_right,
    out_scale,
    own_left,
    own_right,
    add_left,
    add_right,
    send_left,
    send_right,
    got_left,
    right_0,
    right_1,
    gram_send,
    gram_0,
    gram_1,
    roots,
    inverses,
    mixes,
    mix_send,
    got_mix,
    made_right,
    squares,
    rows,
    parts,
    mine_total,
    totals,
    table_vmem,
    table,
    tab,
    sends,
    recvs,
    row_sems,
    locals_,
):
    row, me = lax.axis_index("row"), lax.axis_index("col")
    order, half = got_left.shape[2:]
    wide = 2 * half
    tiles, slots = own_left.shape[0], add_left.shape[0]
    pairs = slots // CAP
    at_tile, at_source, at_used, at_seq, at_has = 0, CAP * n, 2 * CAP * n, 3 * CAP * n, 4 * CAP * n
    at_owner, at_index, at_rank, at_add, at_keep = (5 * CAP * n + i * slots for i in range(5))
    at_arrival = 5 * CAP * n + 5 * slots
    at_hit = at_arrival + tiles
    got_right = (right_0, right_1)
    got_gram = (gram_0, gram_1)

    loads = []
    for i, (src, dst) in enumerate(
        (
            (add_left_hbm, add_left),
            (own_right_hbm, own_right),
            (own_left_hbm, own_left),
            (add_right_hbm, add_right),
        )
    ):
        load = pltpu.make_async_copy(src, dst, locals_.at[9, i])
        load.start()
        loads.append(load)

    barrier = pltpu.get_barrier_semaphore()
    for step in range(1, n):
        pl.semaphore_signal(
            barrier,
            inc=1,
            device_id=(row, lax.rem(me + step, n)),
            device_id_type=pl.DeviceIdType.MESH,
        )
    for step in range(1, m):
        pl.semaphore_signal(
            barrier,
            inc=1,
            device_id=(lax.rem(row + step, m), me),
            device_id_type=pl.DeviceIdType.MESH,
        )

    def slots_of(owner, held):
        count, found = jnp.int32(0), [jnp.int32(0)] * CAP
        for j in range(slots):
            hit = lax.div(held(j), tiles) == owner
            for c in range(CAP):
                found[c] = jnp.where(hit & (count == c), j, found[c])
            count = count + jnp.where(hit, 1, 0)
        return jnp.where(count > 0, 1, 0), found

    def my_owner(o, before):
        has, found = slots_of(o, lambda j: mine[0, j])
        for c in range(CAP):
            tab[at_source + c * n + o] = found[c]
        tab[at_seq + o] = jnp.minimum(before, pairs - 1)
        tab[at_has + o] = has
        return before + has

    lax.fori_loop(0, n, my_owner, jnp.int32(0))

    def pack_left(c):
        def one(o, _):
            send_left[c, o] = add_left[tab[at_source + c * n + o]]
            return 0

        lax.fori_loop(0, n, one, 0)

    loads[0].wait()
    pack_left(0)
    pack_left(1)
    pl.semaphore_wait(barrier, n + m - 2)

    steps = [s for g in range(1, n // 2 + 1) for s in sorted({g, n - g})]

    def to_peer(kind, src, dst, step):
        peer = lax.rem(me + step, n)
        copy = pltpu.make_async_remote_copy(
            src_ref=src(peer),
            dst_ref=dst(me),
            send_sem=sends.at[kind, step],
            recv_sem=recvs.at[kind, step],
            device_id=(row, peer),
            device_id_type=pl.DeviceIdType.MESH,
        )
        copy.start()
        return copy

    def to_self(kind, src, dst):
        own = pltpu.make_async_copy(src(me), dst(me), locals_.at[kind, 0])
        own.start()
        return own

    def exchange(kind, src, dst):
        copies = [to_peer(kind, src, dst, step) for step in steps]
        return to_self(kind, src, dst), copies

    def as_it_arrives(moved, work):
        moved[0].wait()
        work(me)
        for step, copy in zip(steps, moved[1]):
            copy.wait_recv()
            work(lax.rem(me + n - step, n))

    def arrive(moved):
        moved[0].wait()
        for copy in moved[1]:
            copy.wait_recv()

    def sent(moved):
        for copy in moved[1]:
            copy.wait_send()

    def row_of(p):
        return table_vmem.at[p]

    def left_of(c):
        return exchange(c, lambda p: send_left.at[c, p], lambda p: got_left.at[c, p])

    def right_of(c):
        return exchange(2 + c, lambda p: send_right.at[c, p], lambda p: got_right[c].at[p])

    def mix_of(c):
        return exchange(6 + c, lambda p: mix_send.at[c, p], lambda p: got_mix.at[c, p])

    def masks(at):
        cur, add = tab[at_rank + at], tab[at_add + at]
        keeps = []
        for axis in (0, 1):
            i = iota((wide, wide), axis)
            keeps.append(((i < half) & (i < cur)) | ((i >= half) & (i - half < add)))
        return keeps[0] & keeps[1], keeps[0]

    def one_gram(c, d):
        cur = own_left[tab[at_tile + c * n + d]]
        both = jnp.concatenate([cur, got_left[c, d]], axis=1)
        gram_send[c, d] = contract_rows(cur, both).astype(BF16)

    def owner_grams(c, moved):
        src, dst = (lambda p: gram_send.at[c, p]), (lambda p: got_gram[c].at[p])
        copies = []
        moved[0].wait()
        one_gram(c, me)
        own = to_self(4 + c, src, dst)
        before = None
        for step, copy in zip(steps, moved[1]):
            copy.wait_recv()
            one_gram(c, lax.rem(me + n - step, n))
            if before is not None:
                copies.append(to_peer(4 + c, src, dst, n - before))
            before = step
        copies.append(to_peer(4 + c, src, dst, n - before))
        return own, copies

    def right_stack(c, k):
        at = c * pairs + k
        return jnp.concatenate(
            [got_right[c][tab[at_owner + at]], add_right[tab[at_index + at]]], axis=1
        )

    def tile_roots(c, k):
        at = c * pairs + k
        stack = right_stack(c, k)
        keep, keep_row = masks(at)
        diagonal = iota((wide, wide), 0) == iota((wide, wide), 1)
        identity = jnp.where(diagonal, 1.0, 0.0).astype(F32)
        gram = jnp.where(keep, contract_rows(stack, stack), 0.0)
        gram = gram + jnp.where(diagonal & ~keep_row, 1.0, 0.0)
        scale = jnp.sqrt(total(gram * gram))
        root = gram * (1.0 / scale)
        inverse = 1.5 * identity - 0.5 * root
        root = product(split(root), split(inverse))
        for _ in range(ROOTS - 1):
            q, p = split(inverse), split(root)
            middle = split(1.5 * identity - 0.5 * product(q, p))
            root = product(p, middle)
            inverse = product(middle, q)
        roots[at] = root * jnp.sqrt(scale)
        inverses[at] = inverse * lax.rsqrt(scale)

    def tile_core(c, k):
        at = c * pairs + k
        top = got_gram[c][tab[at_owner + at]].astype(F32)
        add = add_left[tab[at_index + at]]
        low = jnp.concatenate([top[:, half:].T, contract_rows(add, add)], axis=1)
        gram = jnp.concatenate([top, low], axis=0)
        gram = jnp.where(masks(at)[0], gram, 0.0)
        root = roots[at]
        s = split(root)
        folded = root[:, :half] + root[:, half:]
        core = product(s, split(product(split(gram), split(folded))))
        y = core * lax.rsqrt(total(core * core) + 1e-06)
        for i in range(SWEEPS):
            if i < SWEEPS - FINE:
                upper = y.astype(BF16)
                inner = contract_rows(upper, upper).astype(BF16)
                y = 1.5 * y - 0.5 * jnp.dot(upper, inner, preferred_element_type=F32)
            else:
                ys = split(y)
                inner = product(ys, ys, (((0,), (0,)), ((), ())))
                y = 1.5 * y - 0.5 * product(ys, split(inner))
        y = split(jnp.where(iota(y.shape, 1) < tab[at_keep + at], y, 0.0))
        mixes[at] = product(s, y).astype(BF16)
        mix = product(split(inverses[at]), y) * math.sqrt(order)
        return mix.astype(BF16)

    def each(c, work, many):
        def some(i, _):
            for j in range(many):
                work(c, i * many + j)
            return 0

        lax.fori_loop(0, pairs // many, some, 0)

    many = 2 if pairs % 2 == 0 else 1
    mixes_right = inverses

    def finish_core(c, k):
        mixes_right[c * pairs + k, :, :half] = tile_core(c, k).astype(F32)

    def right_out(c, k):
        at = c * pairs + k
        mix = mixes_right[at, :, :half].astype(BF16)
        made_right[at] = jnp.dot(
            right_stack(c, k), mix, preferred_element_type=F32
        ).astype(BF16)

    def pack(c):
        def one(o, _):
            mix_send[c, o] = mixes[c * pairs + tab[at_seq + o]]
            return 0

        lax.fori_loop(0, n, one, 0)

    def index_tables():
        for k in range(pairs):

            def one(o, found):
                chosen = (tab[at_has + o] > 0) & (tab[at_seq + o] == k)
                new = [o] + [tab[at_source + c * n + o] for c in range(CAP)]
                return tuple(jnp.where(chosen, a, b) for a, b in zip(new, found))

            found = lax.fori_loop(0, n, one, (jnp.int32(0),) * (CAP + 1))
            for c in range(CAP):
                at, j = c * pairs + k, found[1 + c]
                tile = lax.rem(mine[0, j], tiles)
                tab[at_owner + at] = found[0]
                tab[at_index + at] = j
                tab[at_rank + at] = table[found[0], 0, slots + tile]
                tab[at_keep + at] = table[found[0], 0, slots + tiles + tile]
                tab[at_add + at] = mine[0, slots + 2 * tiles + j]

    def asked_tables():
        def one(d, _):
            has, found = slots_of(me, lambda j: table[d, 0, j])
            for c in range(CAP):
                tab[at_tile + c * n + d] = lax.rem(table[d, 0, found[c]], tiles)
                tab[at_used + c * n + d] = has
            return 0

        lax.fori_loop(0, n, one, 0)

    def arrival_tables():
        def tile(t, _):
            def one(s, found):
                hit = (tab[at_tile + s] == t) & (tab[at_used + s] > 0)
                return jnp.where(hit, s, found[0]), jnp.where(hit, 1, found[1])

            found = lax.fori_loop(0, CAP * n, one, (jnp.int32(0), jnp.int32(0)))
            tab[at_arrival + t] = found[0]
            tab[at_hit + t] = found[1]
            return 0

        lax.fori_loop(0, tiles, tile, 0)

    def pack_right():
        def one(d, _):
            for c in range(CAP):
                send_right[c, d] = own_right[tab[at_tile + c * n + d]]
            return 0

        lax.fori_loop(0, n, one, 0)

    fresh = send_right

    def new_left(c):
        def one(d):
            both = jnp.concatenate([own_left[tab[at_tile + c * n + d]], got_left[c, d]], axis=1)
            made = jnp.dot(both, got_mix[c, d], preferred_element_type=F32)
            fresh[c, d] = made.astype(BF16)

        return one

    def keep_tiles():
        squares[...] = jnp.zeros_like(squares)

        def one(i, _):
            for b in range(BR):
                t = i * BR + b
                s = tab[at_arrival + t]
                hit = tab[at_hit + t] > 0
                limit = jnp.where(hit, 0, mine[0, slots + t])
                column = iota((order, half), 1)
                old = jnp.where(column < limit, own_left[t].astype(F32), 0.0)
                new = fresh[lax.div(s, n), lax.rem(s, n)].astype(F32)
                kept = jnp.where(hit, new, old)
                kept_left[t] = kept.astype(BF16)
                squares[b] += kept * kept
            return 0

        lax.fori_loop(0, tiles // BR, one, 0)
        for b in range(BR):
            sums = lax.dot_general(
                jnp.ones((8, half), F32),
                squares[b],
                (((1,), (1,)), ((), ())),
                precision=lax.Precision.HIGHEST,
                preferred_element_type=F32,
            )
            rows[0, b : b + 1] = sums[:1]

    def local_copy(src, dst, i):
        copy = pltpu.make_async_copy(src, dst, locals_.at[10, i])
        copy.start()
        copy.wait()

    def scale_rows():
        local_copy(rows.at[0], rows.at[1], 0)
        moved = exchange(9, lambda p: rows.at[1], lambda p: parts.at[p])
        arrive(moved)
        row_sum = jnp.sum(parts[...], axis=0)
        mine_total[0] = jnp.broadcast_to(total(row_sum), mine_total.shape[1:])
        local_copy(mine_total.at[0], mine_total.at[1], 1)
        copies = []
        for step in range(1, m):
            copy = pltpu.make_async_remote_copy(
                src_ref=mine_total.at[1],
                dst_ref=totals.at[row],
                send_sem=row_sems.at[0, step],
                recv_sem=row_sems.at[1, step],
                device_id=(lax.rem(row + step, m), me),
                device_id_type=pl.DeviceIdType.MESH,
            )
            copy.start()
            copies.append(copy)
        local_copy(mine_total.at[1], totals.at[row], 2)
        for copy in copies:
            copy.wait()
        everything = jnp.sum(totals[...], axis=0)[:1, :1]
        out_scale[...] = jnp.sqrt(row_sum / (everything * (1.0 / (m * BR * order))))
        sent(moved)

    routes = exchange(8, lambda p: packed, row_of)
    left_a = left_of(0)
    arrive(routes)
    local_copy(table_vmem, table, 3)
    asked_tables()
    loads[1].wait()
    pack_right()
    right_a = right_of(0)
    index_tables()
    arrival_tables()
    loads[2].wait()
    loads[3].wait()
    gram_a = owner_grams(0, left_a)
    right_b = right_of(1)
    arrive(right_a)
    each(0, tile_roots, many)
    arrive(gram_a)
    each(0, finish_core, many)
    pack(0)
    mix_a = mix_of(0)
    left_b = left_of(1)
    each(0, right_out, many)
    arrive(right_b)
    each(1, tile_roots, many)
    sent(right_a)
    sent(right_b)
    as_it_arrives(mix_a, new_left(0))
    gram_b = owner_grams(1, left_b)
    arrive(gram_b)
    each(1, finish_core, many)
    pack(1)
    mix_b = mix_of(1)
    each(1, right_out, many)
    for j in range(slots):
        o = lax.div(mine[0, j], tiles)
        first = tab[at_source + o] == j
        out_right[j] = made_right[tab[at_seq + o] + jnp.where(first, 0, pairs)]
    as_it_arrives(mix_b, new_left(1))
    keep_tiles()
    scale_rows()
    for moved in (routes, left_a, left_b, gram_a, gram_b, mix_a, mix_b):
        sent(moved)


def sweep(packed, own_left, own_right, add_left, add_right, n, m):
    tiles, order, half = own_left.shape
    slots = add_left.shape[0]
    wide = 2 * half
    vmem = pl.BlockSpec(memory_space=pltpu.VMEM)
    hbm = pl.BlockSpec(memory_space=pl.ANY)
    entries = 5 * CAP * n + 5 * slots + 2 * tiles
    return pl.pallas_call(
        functools.partial(sweep_kernel, n, m),
        in_specs=[pl.BlockSpec(memory_space=pltpu.SMEM), vmem] + [hbm] * 4,
        out_specs=[vmem] * 3,
        out_shape=[
            jax.ShapeDtypeStruct((tiles, order, half), BF16),
            jax.ShapeDtypeStruct((slots, order, half), BF16),
            jax.ShapeDtypeStruct((BR, order), F32),
        ],
        scratch_shapes=[
            pltpu.VMEM((tiles, order, half), BF16),
            pltpu.VMEM((tiles, order, half), BF16),
            pltpu.VMEM((slots, order, half), BF16),
            pltpu.VMEM((slots, order, half), BF16),
            pltpu.VMEM((CAP, n, order, half), BF16),
            pltpu.VMEM((CAP, n, order, half), BF16),
            pltpu.VMEM((CAP, n, order, half), BF16),
            pltpu.VMEM((n, order, half), BF16),
            pltpu.VMEM((n, order, half), BF16),
            pltpu.VMEM((CAP, n, half, wide), BF16),
            pltpu.VMEM((n, half, wide), BF16),
            pltpu.VMEM((n, half, wide), BF16),
            pltpu.VMEM((slots, wide, wide), F32),
            pltpu.VMEM((slots, wide, wide), F32),
            pltpu.VMEM((slots, wide, half), BF16),
            pltpu.VMEM((CAP, n, wide, half), BF16),
            pltpu.VMEM((CAP, n, wide, half), BF16),
            pltpu.VMEM((slots, order, half), BF16),
            pltpu.VMEM((BR, order, half), F32),
            pltpu.VMEM((2, BR, order), F32),
            pltpu.VMEM((n, BR, order), F32),
            pltpu.VMEM((2, 8, 128), F32),
            pltpu.VMEM((m, 8, 128), F32),
            pltpu.VMEM((n,) + packed.shape, jnp.int32),
            pltpu.SMEM((n,) + packed.shape, jnp.int32),
            pltpu.SMEM((entries,), jnp.int32),
            pltpu.SemaphoreType.DMA((10, n)),
            pltpu.SemaphoreType.DMA((10, n)),
            pltpu.SemaphoreType.DMA((2, m)),
            pltpu.SemaphoreType.DMA((11, 4)),
        ],
        compiler_params=pltpu.CompilerParams(
            collective_id=0, has_side_effects=True, vmem_limit_bytes=62 * 1024 * 1024
        ),
        name="sweep",
    )(packed, packed, own_left, own_right, add_left, add_right)


def local(
    current_left,
    current_right,
    current_rank,
    target_rank,
    update_left,
    update_right,
    update_rank,
    owner_slot,
):
    packed = jnp.concatenate([owner_slot, current_rank, target_rank, update_rank], axis=1)
    width = -(-packed.shape[1] // 128) * 128
    packed = jnp.pad(packed, ((0, 0), (0, width - packed.shape[1])))
    kept, right, scale = sweep(
        packed,
        current_left[0],
        current_right[0],
        update_left[0],
        update_right[0],
        lax.axis_size("col"),
        lax.axis_size("row"),
    )
    return (kept[None], right[None], scale)


def solution(mesh):
    return jax.shard_map(
        local,
        mesh=mesh,
        in_specs=(
            P("row", "col", None, None),
            P("row", "col", None, None),
            P("row", "col"),
            P("row", "col"),
            P("row", "col", None, None),
            P("row", "col", None, None),
            P("row", "col"),
            P("row", "col"),
        ),
        out_specs=(P("row", "col", None, None), P("row", "col", None, None), P("row", None)),
        check_vma=False,
    )
```
